32 devices in a mesh: section: 16 (over z, y, core), dp: 2 (over x).
Axes of the slice: x: 2, y: 2, z: 4, core: 2. Of those that a mesh axis runs over, the one named last changes fastest.
Arguments:
- activations: bfloat16 [16, 16, 64, 4096], P('section', 'dp'), may hold values from -6 to 6
- out_grads: bfloat16 [16, 16, 64, 4096], P('section', 'dp'), may hold values from -6 to 6
- proj_in: bfloat16 [16, 2, 4096, 128], P('section'), may hold values from -0.09375 to 0.09375
- proj_out: bfloat16 [16, 2, 64, 4096], P('section'), may hold values from -0.09375 to 0.09375
- earlier_gram: float32 [8192, 8192], P('section', 'dp'), may hold values from -4 to 4, as said below
Outputs:
- gram: float32 [8192, 8192], P('section', 'dp')
The draws below stay inside these ranges and needn't reach their ends.
Inputs may be any that keep to these rules, and one draw needn't show every extreme that they name: earlier_gram is symmetric.
All inputs are finite; a program needn't handle non-finite values.
Results may differ from the reference program's by a relative error of at most 0.0013.
Values sent between devices are 32-bit elements; how exact they have to be, the bound alone decides.
A program may use at most 64 MiB of HBM per device.

```python
import math
import jax
import jax.numpy as jnp
from jax import lax

D = 4096
K_IN = 128
K_OUT = 64
PROJ = 2
LEN = 64
LAYERS = 16
EXAMPLES = 16
K = 8192


def draw_earlier_gram(key, part):
    noise = jax.random.normal(jax.random.fold_in(key, 17), (K, K), jnp.float32)
    return jnp.clip((noise + noise.T) * 0.5, -4.0, 4.0)


def steps_of(stream_key, shape, cuts, least, largest):
    gain = 1.0
    for position, parts in cuts:
        heights = jax.random.uniform(jax.random.fold_in(jax.random.fold_in(stream_key, 6), position), (parts,), jnp.float32, least / len(cuts), largest / len(cuts))
        gain = gain * jnp.repeat(jnp.exp(heights), shape[position] // parts).reshape((-1,) + (1,) * (len(shape) - 1 - position))
    return gain


def centred(rng, shape, deviation, most, shards=(), kind=jnp.bfloat16):
    drawn = deviation * jax.random.normal(rng, shape, jnp.float32)
    if shards:
        drawn = drawn * steps_of(rng, shape, shards, -0.22, 0.18)
    return jnp.clip(drawn, -most, most).astype(kind)


def setup_inputs(seed: int = 0) -> dict:
    key_list = jax.random.split(jax.random.key(seed), 6)
    return {
        "activations": centred(key_list[0], (LAYERS, EXAMPLES, LEN, D), 1.0, 6.0, ((0, 16), (1, 2))),
        "out_grads": centred(key_list[1], (LAYERS, EXAMPLES, LEN, D), 1.0, 6.0, ((0, 16), (1, 2))),
        "proj_in": centred(key_list[2], (LAYERS, PROJ, D, K_IN), D ** -0.5, 0.09375, ((0, 16),)),
        "proj_out": centred(key_list[3], (LAYERS, PROJ, K_OUT, D), D ** -0.5, 0.09375, ((0, 16),)),
        "earlier_gram": draw_earlier_gram(jax.random.fold_in(key_list[5], 71), 0),
    }


def reference(activations, out_grads, proj_in, proj_out, earlier_gram):

    def layer_step(total, inputs):
        layer_act, layer_grad, layer_in, layer_out = inputs
        low_in = jnp.einsum('eld,pdm->pelm', layer_act.astype(jnp.float32), layer_in.astype(jnp.float32)).astype(jnp.bfloat16)
        low_out = jnp.einsum('pkd,eld->pekl', layer_out.astype(jnp.float32), layer_grad.astype(jnp.float32)).astype(jnp.bfloat16)
        partial_terms = jnp.einsum('pekl,pelm->ekm', low_out.astype(jnp.float32), low_in.astype(jnp.float32))
        return (total + partial_terms.reshape(partial_terms.shape[0], -1), None)
    start = jnp.zeros((EXAMPLES, K_OUT * K_IN), jnp.float32)
    summed, unused = lax.scan(layer_step, start, (activations, out_grads, proj_in, proj_out))
    features = summed / math.sqrt(LEN * LAYERS * PROJ)
    outer = jnp.dot(features.T, features, precision=lax.Precision.HIGHEST)
    return earlier_gram + outer / EXAMPLES
```

```python
import functools
import math

import jax
import jax.numpy as jnp
from jax import lax
from jax.experimental import pallas as pl
from jax.experimental.pallas import tpu as pltpu
from jax.sharding import PartitionSpec as P

MESH = pl.DeviceIdType.MESH
LANES = 128
HALVES = 2
DEPTHS = 4


def split(x):
    hi = x.astype(jnp.bfloat16)
    lo = (x - hi.astype(jnp.float32)).astype(jnp.bfloat16)
    return hi, lo


def feature_kernel(
    n, groups, count, scale,
    act, grad, p_in, p_out,
    left, right,
    act_v, grad_v, in_v, out_v, low_in, low_out,
    mine, theirs, arrived, pieces, whole, cols, row,
    load_sem, pair_sem, send_sem, recv_sem, dp_send, dp_recv,
    col_send, col_recv, fwd_send, row_sem,
):
    s = lax.axis_index("section")
    d = lax.axis_index("dp")
    chips = n // 2
    core = s % 2
    chip = s // 2
    partner = s + 1 - 2 * core

    draws, width, k_in = p_in.shape
    k_out = p_out.shape[1]
    tokens = act.shape[0]
    length = tokens // count
    rows = tokens // HALVES
    depth = width // DEPTHS

    loads = {}
    slot = 0
    for h in range(HALVES):
        for c in range(DEPTHS):
            cs = pl.ds(c * depth, depth)
            rs = pl.ds(h * rows, rows)
            wanted = []
            if h == 0:
                wanted.append(("p_in", p_in.at[:, cs], in_v.at[:, cs]))
            wanted.append(("act", act.at[rs, cs], act_v.at[rs, cs]))
            if h == 0:
                wanted.append(("p_out", p_out.at[:, :, cs], out_v.at[:, :, cs]))
            wanted.append(("grad", grad.at[rs, cs], grad_v.at[rs, cs]))
            for name, src, dst in wanted:
                copy = pltpu.make_async_copy(src, dst, load_sem.at[slot])
                copy.start()
                loads[name, h, c] = copy
                slot += 1

    barrier = pltpu.get_barrier_semaphore()
    for i in range(1, n):
        pl.semaphore_signal(barrier, inc=1, device_id={"section": (s + i) % n, "dp": d}, device_id_type=MESH)
    for j in range(1, groups):
        pl.semaphore_signal(barrier, inc=1, device_id={"section": s, "dp": (d + j) % groups}, device_id_type=MESH)

    for h in range(HALVES):
        rs = slice(h * rows, (h + 1) * rows)
        total_in = total_out = None
        for c in range(DEPTHS):
            cs = slice(c * depth, (c + 1) * depth)
            if h == 0:
                loads["p_in", h, c].wait()
            loads["act", h, c].wait()
            weights = jnp.concatenate([in_v[p, cs, :] for p in range(draws)], axis=1)
            term = jnp.dot(act_v[rs, cs], weights, preferred_element_type=jnp.float32)
            total_in = term if total_in is None else total_in + term
            if h == 0:
                loads["p_out", h, c].wait()
            loads["grad", h, c].wait()
            weights = out_v[:, :, cs].reshape(draws * k_out, depth)
            term = lax.dot_general(
                grad_v[rs, cs], weights, (((1,), (1,)), ((), ())), preferred_element_type=jnp.float32
            )
            total_out = term if total_out is None else total_out + term
        low_in[rs, :] = total_in.astype(jnp.bfloat16)
        low_out[:, rs] = total_out.T.astype(jnp.bfloat16)

    k_half = k_out // 2

    def terms(which, into):
        for e in range(count):
            ts = slice(e * length, (e + 1) * length)
            value = None
            for p in range(draws):
                start = pl.multiple_of(p * k_out + which * k_half, k_half)
                term = jnp.dot(
                    low_out[pl.ds(start, k_half), ts],
                    low_in[ts, p * k_in:(p + 1) * k_in],
                    preferred_element_type=jnp.float32,
                )
                value = term if value is None else value + term
            into[:, e, :] = value

    def remote(src, dst, ssem, rsem, section, dp):
        return pltpu.make_async_remote_copy(
            src_ref=src, dst_ref=dst, send_sem=ssem, recv_sem=rsem,
            device_id={"section": section, "dp": dp}, device_id_type=MESH,
        )

    terms(1 - core, theirs)
    pl.semaphore_wait(barrier, n - 1 + groups - 1)
    swap = remote(theirs, arrived, pair_sem.at[0], pair_sem.at[1], partner, d)
    swap.start()
    terms(core, mine)
    swap.wait_recv()

    k_chunk = k_half // chips
    sends = []
    for i in range(chips - 1, 0, -1):
        to = (chip + i) % chips
        ks = pl.ds(to * k_chunk, k_chunk)
        mine[ks] = mine[ks] + arrived[ks]
        copy = remote(mine.at[ks], pieces.at[i - 1], send_sem.at[i - 1], recv_sem.at[i - 1], 2 * to + core, d)
        copy.start()
        sends.append(copy)
    ks = pl.ds(chip * k_chunk, k_chunk)
    total = mine[ks] + arrived[ks]
    for i in range(1, chips):
        sends[chips - 1 - i].wait_recv()
        total = total + pieces[i - 1]

    def block(g):
        return pl.ds(pl.multiple_of(g * count, count), count)

    whole[:, block(d), :] = total
    for j in range(1, groups):
        to = (d + j) % groups
        copy = remote(whole.at[:, block(d), :], whole.at[:, block(d), :], dp_send.at[j - 1], dp_recv.at[j - 1], s, to)
        copy.start()
        sends.append(copy)
    for j in range(1, groups):
        origin = (d + groups - j) % groups
        remote(
            whole.at[:, block(origin), :], whole.at[:, block(origin), :], dp_send.at[j - 1], dp_recv.at[j - 1], s, origin
        ).wait_recv()

    per_group = n // groups
    q = core * chips + chip
    own_slot = q % per_group
    is_col = q // per_group == d

    def col_copies():
        copies = [remote(whole, cols.at[own_slot], col_send.at[0], col_recv.at[own_slot], partner, d)]
        for i in range(1, chips):
            to = 2 * ((chip + i) % chips) + core
            copies.append(remote(whole, cols.at[own_slot], col_send.at[i], col_recv.at[own_slot], to, d))
        return copies

    def row_copy():
        return remote(whole, row, row_sem.at[0], row_sem.at[1], q, d)

    @pl.when(is_col)
    def _():
        for copy in col_copies():
            copy.start()
        cols[own_slot] = whole[...]

    @pl.when(jnp.logical_and(jnp.logical_not(is_col), q != s))
    def _():
        row_copy().start()

    @pl.when(jnp.logical_and(jnp.logical_not(is_col), q == s))
    def _():
        row[...] = whole[...]

    def forward(j):
        return remote(cols.at[j], cols.at[j], fwd_send.at[j], col_recv.at[j], partner, d)

    for i in range(per_group):
        j = (chip + per_group * chips - i) % per_group
        owner = d * per_group + j
        owner_core = owner // chips

        @pl.when(owner != q)
        def _():
            forward(j).wait_recv()

        @pl.when(jnp.logical_and(owner != q, owner_core == core))
        def _():
            forward(j).start()

        for k in range(k_chunk):
            hi, lo = split(cols[j, k])
            at = pl.multiple_of((j * k_chunk + k) * LANES, LANES)
            right[:, pl.ds(at, LANES)] = jnp.concatenate([hi, hi, lo], axis=0)

    @pl.when(jnp.logical_and(s // per_group != d, q != s))
    def _():
        row_copy().wait_recv()

    @pl.when(s // per_group == d)
    def _():
        row[...] = cols[s % per_group]

    for k in range(k_chunk):
        hi, lo = split(row[k] * scale)
        left[:, k * LANES:(k + 1) * LANES] = jnp.concatenate([hi, lo, hi], axis=0)

    swap.wait_send()
    for copy in sends:
        copy.wait_send()

    @pl.when(is_col)
    def _():
        for copy in col_copies():
            copy.wait_send()

    @pl.when(jnp.logical_and(jnp.logical_not(is_col), q != s))
    def _():
        row_copy().wait_send()

    for j in range(per_group):
        owner = d * per_group + j

        @pl.when(jnp.logical_and(owner != q, owner // chips == core))
        def _():
            forward(j).wait_send()


def gram_kernel(tiles, left, right, earlier, out, tile_v, sem):
    columns = right.shape[1] // tiles
    lhs = left[...].T
    copies = []
    for i in range(tiles):
        cs = slice(i * columns, (i + 1) * columns)
        tile_v[:, cs] = earlier[:, cs] + jnp.dot(lhs, right[:, cs], preferred_element_type=jnp.float32)
        copy = pltpu.make_async_copy(
            tile_v.at[:, pl.ds(i * columns, columns)], out.at[:, pl.ds(i * columns, columns)], sem.at[i]
        )
        copy.start()
        copies.append(copy)
    for copy in copies:
        copy.wait()


def per_device(activations, out_grads, proj_in, proj_out, earlier_gram):
    n = lax.axis_size("section")
    groups = lax.axis_size("dp")
    _, count, length, width = activations.shape
    _, draws, _, k_in = proj_in.shape
    k_out = proj_out.shape[2]
    tokens = count * length
    examples = count * groups
    scale = 1.0 / (length * n * draws) / examples
    row_width, col_width = earlier_gram.shape
    chips = n // 2
    k_half = k_out // 2
    k_chunk = k_half // chips
    per_group = n // groups
    any_spec = pl.BlockSpec(memory_space=pl.ANY)
    vmem_spec = pl.BlockSpec(memory_space=pltpu.VMEM)
    f32, bf16 = jnp.float32, jnp.bfloat16
    dma = pltpu.SemaphoreType.DMA

    left, right = pl.pallas_call(
        functools.partial(feature_kernel, n, groups, count, scale),
        out_shape=(
            jax.ShapeDtypeStruct((3 * examples, row_width), bf16),
            jax.ShapeDtypeStruct((3 * examples, col_width), bf16),
        ),
        in_specs=[pl.BlockSpec(memory_space=pltpu.HBM)] * 4,
        out_specs=(vmem_spec, vmem_spec),
        scratch_shapes=[
            pltpu.VMEM((tokens, width), bf16),
            pltpu.VMEM((tokens, width), bf16),
            pltpu.VMEM((draws, width, k_in), bf16),
            pltpu.VMEM((draws, k_out, width), bf16),
            pltpu.VMEM((tokens, draws * k_in), bf16),
            pltpu.VMEM((draws * k_out, tokens), bf16),
            pltpu.VMEM((k_half, count, k_in), f32),
            pltpu.VMEM((k_half, count, k_in), f32),
            pltpu.VMEM((k_half, count, k_in), f32),
            pltpu.VMEM((chips - 1, k_chunk, count, k_in), f32),
            pltpu.VMEM((k_chunk, examples, k_in), f32),
            pltpu.VMEM((per_group, k_chunk, examples, k_in), f32),
            pltpu.VMEM((k_chunk, examples, k_in), f32),
            dma((2 * DEPTHS * (HALVES + 1),)),
            dma((2,)),
            dma((chips - 1,)),
            dma((chips - 1,)),
            dma((groups - 1,)),
            dma((groups - 1,)),
            dma((chips,)),
            dma((per_group,)),
            dma((per_group,)),
            dma((2,)),
        ],
        compiler_params=pltpu.CompilerParams(
            collective_id=0, has_side_effects=True, vmem_limit_bytes=28 << 20
        ),
        name="features",
    )(
        activations.reshape(tokens, width),
        out_grads.reshape(tokens, width),
        proj_in[0],
        proj_out[0],
    )
    tiles = 8
    return pl.pallas_call(
        functools.partial(gram_kernel, tiles),
        out_shape=jax.ShapeDtypeStruct((row_width, col_width), f32),
        in_specs=[vmem_spec, vmem_spec, vmem_spec],
        out_specs=any_spec,
        scratch_shapes=[pltpu.VMEM((row_width, col_width), f32), dma((tiles,))],
        compiler_params=pltpu.CompilerParams(vmem_limit_bytes=28 << 20),
        name="gram",
    )(left, right, earlier_gram)


def solution(mesh):
    return jax.shard_map(
        per_device,
        mesh=mesh,
        in_specs=(
            P("section", "dp", None, None),
            P("section", "dp", None, None),
            P("section", None, None, None),
            P("section", None, None, None),
            P("section", "dp"),
        ),
        out_specs=P("section", "dp"),
        check_vma=False,
    )
```

```python
import functools
import math

import jax
import jax.numpy as jnp
from jax import lax
from jax.experimental import pallas as pl
from jax.experimental.pallas import tpu as pltpu
from jax.sharding import PartitionSpec as P

MESH = pl.DeviceIdType.MESH
LANES = 128
HALVES = 2
DEPTHS = 4


def split(x):
    hi = x.astype(jnp.bfloat16)
    lo = (x - hi.astype(jnp.float32)).astype(jnp.bfloat16)
    return hi, lo


def feature_kernel(
    n, groups, count, scale,
    act, grad, p_in, p_out,
    left, right,
    act_v, grad_v, in_v, out_v, low_in, low_out,
    mine, theirs, arrived, pieces, whole, cols, row,
    load_sem, pair_sem, send_sem, recv_sem, dp_send, dp_recv,
    col_send, col_recv, fwd_send, row_sem,
):
    s = lax.axis_index("section")
    d = lax.axis_index("dp")
    chips = n // 2
    core = s % 2
    chip = s // 2
    partner = s + 1 - 2 * core

    draws, width, k_in = p_in.shape
    k_out = p_out.shape[1]
    tokens = act.shape[0]
    length = tokens // count
    rows = tokens // HALVES
    depth = width // DEPTHS

    loads = {}
    slot = 0
    for h in range(HALVES):
        for c in range(DEPTHS):
            cs = pl.ds(c * depth, depth)
            rs = pl.ds(h * rows, rows)
            wanted = []
            if h == 0:
                wanted.append(("p_in", p_in.at[:, cs], in_v.at[:, cs]))
            wanted.append(("act", act.at[rs, cs], act_v.at[rs, cs]))
            if h == 0:
                wanted.append(("p_out", p_out.at[:, :, cs], out_v.at[:, :, cs]))
            wanted.append(("grad", grad.at[rs, cs], grad_v.at[rs, cs]))
            for name, src, dst in wanted:
                copy = pltpu.make_async_copy(src, dst, load_sem.at[slot])
                copy.start()
                loads[name, h, c] = copy
                slot += 1

    barrier = pltpu.get_barrier_semaphore()
    for i in range(1, n):
        pl.semaphore_signal(barrier, inc=1, device_id={"section": (s + i) % n, "dp": d}, device_id_type=MESH)
    for j in range(1, groups):
        pl.semaphore_signal(barrier, inc=1, device_id={"section": s, "dp": (d + j) % groups}, device_id_type=MESH)

    for h in range(HALVES):
        rs = slice(h * rows, (h + 1) * rows)
        total_in = total_out = None
        for c in range(DEPTHS):
            cs = slice(c * depth, (c + 1) * depth)
            if h == 0:
                loads["p_in", h, c].wait()
            loads["act", h, c].wait()
            weights = jnp.concatenate([in_v[p, cs, :] for p in range(draws)], axis=1)
            term = jnp.dot(act_v[rs, cs], weights, preferred_element_type=jnp.float32)
            total_in = term if total_in is None else total_in + term
            if h == 0:
                loads["p_out", h, c].wait()
            loads["grad", h, c].wait()
            weights = out_v[:, :, cs].reshape(draws * k_out, depth)
            term = lax.dot_general(
                grad_v[rs, cs], weights, (((1,), (1,)), ((), ())), preferred_element_type=jnp.float32
            )
            total_out = term if total_out is None else total_out + term
        low_in[rs, :] = total_in.astype(jnp.bfloat16)
        low_out[:, rs] = total_out.T.astype(jnp.bfloat16)

    k_half = k_out // 2

    def terms(which, into):
        for e in range(count):
            ts = slice(e * length, (e + 1) * length)
            value = None
            for p in range(draws):
                start = pl.multiple_of(p * k_out + which * k_half, k_half)
                term = jnp.dot(
                    low_out[pl.ds(start, k_half), ts],
                    low_in[ts, p * k_in:(p + 1) * k_in],
                    preferred_element_type=jnp.float32,
                )
                value = term if value is None else value + term
            into[:, e, :] = value

    def remote(src, dst, ssem, rsem, section, dp):
        return pltpu.make_async_remote_copy(
            src_ref=src, dst_ref=dst, send_sem=ssem, recv_sem=rsem,
            device_id={"section": section, "dp": dp}, device_id_type=MESH,
        )

    terms(1 - core, theirs)
    pl.semaphore_wait(barrier, n - 1 + groups - 1)
    swap = remote(theirs, arrived, pair_sem.at[0], pair_sem.at[1], partner, d)
    swap.start()
    terms(core, mine)
    swap.wait_recv()

    k_chunk = k_half // chips
    sends = []
    for i in range(chips - 1, 0, -1):
        to = (chip + i) % chips
        ks = pl.ds(to * k_chunk, k_chunk)
        mine[ks] = mine[ks] + arrived[ks]
        copy = remote(mine.at[ks], pieces.at[i - 1], send_sem.at[i - 1], recv_sem.at[i - 1], 2 * to + core, d)
        copy.start()
        sends.append(copy)
    ks = pl.ds(chip * k_chunk, k_chunk)
    total = mine[ks] + arrived[ks]
    for i in range(1, chips):
        sends[chips - 1 - i].wait_recv()
        total = total + pieces[i - 1]

    def block(g):
        return pl.ds(pl.multiple_of(g * count, count), count)

    whole[:, block(d), :] = total
    for j in range(1, groups):
        to = (d + j) % groups
        copy = remote(whole.at[:, block(d), :], whole.at[:, block(d), :], dp_send.at[j - 1], dp_recv.at[j - 1], s, to)
        copy.start()
        sends.append(copy)
    for j in range(1, groups):
        origin = (d + groups - j) % groups
        remote(
            whole.at[:, block(origin), :], whole.at[:, block(origin), :], dp_send.at[j - 1], dp_recv.at[j - 1], s, origin
        ).wait_recv()

    per_group = n // groups
    q = core * chips + chip
    own_slot = q % per_group
    is_col = q // per_group == d

    def col_copies():
        copies = [remote(whole, cols.at[own_slot], col_send.at[0], col_recv.at[own_slot], partner, d)]
        for i in range(1, chips):
            to = 2 * ((chip + i) % chips) + core
            copies.append(remote(whole, cols.at[own_slot], col_send.at[i], col_recv.at[own_slot], to, d))
        return copies

    def row_copy():
        return remote(whole, row, row_sem.at[0], row_sem.at[1], q, d)

    @pl.when(is_col)
    def _():
        for copy in col_copies():
            copy.start()
        cols[own_slot] = whole[...]

    @pl.when(jnp.logical_and(jnp.logical_not(is_col), q != s))
    def _():
        row_copy().start()

    @pl.when(jnp.logical_and(jnp.logical_not(is_col), q == s))
    def _():
        row[...] = whole[...]

    def forward(j):
        return remote(cols.at[j], cols.at[j], fwd_send.at[j], col_recv.at[j], partner, d)

    for i in range(per_group):
        j = (chip + per_group * chips - i) % per_group
        owner = d * per_group + j
        owner_core = owner // chips

        @pl.when(owner != q)
        def _():
            forward(j).wait_recv()

        @pl.when(jnp.logical_and(owner != q, owner_core == core))
        def _():
            forward(j).start()

        for k in range(k_chunk):
            hi, lo = split(cols[j, k])
            at = pl.multiple_of((j * k_chunk + k) * LANES, LANES)
            right[:, pl.ds(at, LANES)] = jnp.concatenate([hi, hi, lo], axis=0)

    @pl.when(jnp.logical_and(s // per_group != d, q != s))
    def _():
        row_copy().wait_recv()

    @pl.when(s // per_group == d)
    def _():
        row[...] = cols[s % per_group]

    for k in range(k_chunk):
        hi, lo = split(row[k] * scale)
        left[:, k * LANES:(k + 1) * LANES] = jnp.concatenate([hi, lo, hi], axis=0)

    swap.wait_send()
    for copy in sends:
        copy.wait_send()

    @pl.when(is_col)
    def _():
        for copy in col_copies():
            copy.wait_send()

    @pl.when(jnp.logical_and(jnp.logical_not(is_col), q != s))
    def _():
        row_copy().wait_send()

    for j in range(per_group):
        owner = d * per_group + j

        @pl.when(jnp.logical_and(owner != q, owner // chips == core))
        def _():
            forward(j).wait_send()


def gram_kernel(tiles, left, right, earlier, out, tile_v, sem):
    columns = right.shape[1] // tiles
    lhs = left[...].T
    copies = []
    for i in range(tiles):
        cs = slice(i * columns, (i + 1) * columns)
        tile_v[:, cs] = earlier[:, cs] + jnp.dot(lhs, right[:, cs], preferred_element_type=jnp.float32)
        copy = pltpu.make_async_copy(
            tile_v.at[:, pl.ds(i * columns, columns)], out.at[:, pl.ds(i * columns, columns)], sem.at[i]
        )
        copy.start()
        copies.append(copy)
    for copy in copies:
        copy.wait()


def per_device(activations, out_grads, proj_in, proj_out, earlier_gram):
    n = lax.axis_size("section")
    groups = lax.axis_size("dp")
    _, count, length, width = activations.shape
    _, draws, _, k_in = proj_in.shape
    k_out = proj_out.shape[2]
    tokens = count * length
    examples = count * groups
    scale = 1.0 / (length * n * draws) / examples
    row_width, col_width = earlier_gram.shape
    chips = n // 2
    k_half = k_out // 2
    k_chunk = k_half // chips
    per_group = n // groups
    any_spec = pl.BlockSpec(memory_space=pl.ANY)
    vmem_spec = pl.BlockSpec(memory_space=pltpu.VMEM)
    f32, bf16 = jnp.float32, jnp.bfloat16
    dma = pltpu.SemaphoreType.DMA

    left, right = pl.pallas_call(
        functools.partial(feature_kernel, n, groups, count, scale),
        out_shape=(
            jax.ShapeDtypeStruct((3 * examples, row_width), bf16),
            jax.ShapeDtypeStruct((3 * examples, col_width), bf16),
        ),
        in_specs=[any_spec] * 4,
        out_specs=(vmem_spec, vmem_spec),
        scratch_shapes=[
            pltpu.VMEM((tokens, width), bf16),
            pltpu.VMEM((tokens, width), bf16),
            pltpu.VMEM((draws, width, k_in), bf16),
            pltpu.VMEM((draws, k_out, width), bf16),
            pltpu.VMEM((tokens, draws * k_in), bf16),
            pltpu.VMEM((draws * k_out, tokens), bf16),
            pltpu.VMEM((k_half, count, k_in), f32),
            pltpu.VMEM((k_half, count, k_in), f32),
            pltpu.VMEM((k_half, count, k_in), f32),
            pltpu.VMEM((chips - 1, k_chunk, count, k_in), f32),
            pltpu.VMEM((k_chunk, examples, k_in), f32),
            pltpu.VMEM((per_group, k_chunk, examples, k_in), f32),
            pltpu.VMEM((k_chunk, examples, k_in), f32),
            dma((2 * DEPTHS * (HALVES + 1),)),
            dma((2,)),
            dma((chips - 1,)),
            dma((chips - 1,)),
            dma((groups - 1,)),
            dma((groups - 1,)),
            dma((chips,)),
            dma((per_group,)),
            dma((per_group,)),
            dma((2,)),
        ],
        compiler_params=pltpu.CompilerParams(
            collective_id=0, has_side_effects=True, vmem_limit_bytes=53 << 20
        ),
        name="features",
    )(
        activations.reshape(tokens, width),
        out_grads.reshape(tokens, width),
        proj_in[0],
        proj_out[0],
    )
    tiles = 8
    return pl.pallas_call(
        functools.partial(gram_kernel, tiles),
        out_shape=jax.ShapeDtypeStruct((row_width, col_width), f32),
        in_specs=[vmem_spec, vmem_spec, vmem_spec],
        out_specs=any_spec,
        scratch_shapes=[pltpu.VMEM((row_width, col_width), f32), dma((tiles,))],
        compiler_params=pltpu.CompilerParams(vmem_limit_bytes=28 << 20),
        name="gram",
    )(left, right, earlier_gram)


def solution(mesh):
    return jax.shard_map(
        per_device,
        mesh=mesh,
        in_specs=(
            P("section", "dp", None, None),
            P("section", "dp", None, None),
            P("section", None, None, None),
            P("section", None, None, None),
            P("section", "dp"),
        ),
        out_specs=P("section", "dp"),
        check_vma=False,
    )
```

```python
import functools
import math

import jax
import jax.numpy as jnp
from jax import lax
from jax.experimental import pallas as pl
from jax.experimental.pallas import tpu as pltpu
from jax.sharding import PartitionSpec as P

MESH = pl.DeviceIdType.MESH
LANES = 128
HALVES = 2
DEPTHS = 4


def split(x):
    hi = x.astype(jnp.bfloat16)
    lo = (x - hi.astype(jnp.float32)).astype(jnp.bfloat16)
    return hi, lo


def feature_kernel(
    n, groups, count, scale,
    act, grad, p_in, p_out, earlier,
    left, right, held,
    act_v, grad_v, in_v, out_v, low_in, low_out,
    mine, theirs, arrived, pieces, own, cols, row,
    load_sem, pair_sem, send_sem, recv_sem,
    col_send, col_recv, fwd_send, row_send, row_recv, held_sem,
):
    s = lax.axis_index("section")
    d = lax.axis_index("dp")
    chips = n // 2
    core = s % 2
    chip = s // 2
    partner = s + 1 - 2 * core

    draws, width, k_in = p_in.shape
    k_out = p_out.shape[1]
    tokens = act.shape[0]
    length = tokens // count
    rows = tokens // HALVES
    depth = width // DEPTHS

    loads = {}
    slot = 0
    for h in range(HALVES):
        for c in range(DEPTHS):
            cs = pl.ds(c * depth, depth)
            rs = pl.ds(h * rows, rows)
            wanted = []
            if h == 0:
                wanted.append(("p_in", p_in.at[:, cs], in_v.at[:, cs]))
            wanted.append(("act", act.at[rs, cs], act_v.at[rs, cs]))
            if h == 0:
                wanted.append(("p_out", p_out.at[:, :, cs], out_v.at[:, :, cs]))
            wanted.append(("grad", grad.at[rs, cs], grad_v.at[rs, cs]))
            for name, src, dst in wanted:
                copy = pltpu.make_async_copy(src, dst, load_sem.at[slot])
                copy.start()
                loads[name, h, c] = copy
                slot += 1

    barrier = pltpu.get_barrier_semaphore()
    for g in range(groups):
        for i in range(n):
            if g or i:
                peer = {"section": (s + i) % n, "dp": (d + g) % groups}
                pl.semaphore_signal(barrier, inc=1, device_id=peer, device_id_type=MESH)

    for h in range(HALVES):
        rs = slice(h * rows, (h + 1) * rows)
        total_in = total_out = None
        for c in range(DEPTHS):
            cs = slice(c * depth, (c + 1) * depth)
            if h == 0:
                loads["p_in", h, c].wait()
            loads["act", h, c].wait()
            weights = jnp.concatenate([in_v[p, cs, :] for p in range(draws)], axis=1)
            term = jnp.dot(act_v[rs, cs], weights, preferred_element_type=jnp.float32)
            total_in = term if total_in is None else total_in + term
            if h == 0:
                loads["p_out", h, c].wait()
            loads["grad", h, c].wait()
            weights = out_v[:, :, cs].reshape(draws * k_out, depth)
            term = lax.dot_general(
                grad_v[rs, cs], weights, (((1,), (1,)), ((), ())), preferred_element_type=jnp.float32
            )
            total_out = term if total_out is None else total_out + term
        if h == HALVES - 1:
            hold = pltpu.make_async_copy(earlier, held, held_sem)
            hold.start()
        low_in[rs, :] = total_in.astype(jnp.bfloat16)
        low_out[:, rs] = total_out.T.astype(jnp.bfloat16)

    k_half = k_out // 2

    def terms(which, into):
        for e in range(count):
            ts = slice(e * length, (e + 1) * length)
            value = None
            for p in range(draws):
                start = pl.multiple_of(p * k_out + which * k_half, k_half)
                term = jnp.dot(
                    low_out[pl.ds(start, k_half), ts],
                    low_in[ts, p * k_in:(p + 1) * k_in],
                    preferred_element_type=jnp.float32,
                )
                value = term if value is None else value + term
            into[:, e, :] = value

    def remote(src, dst, ssem, rsem, section, dp):
        return pltpu.make_async_remote_copy(
            src_ref=src, dst_ref=dst, send_sem=ssem, recv_sem=rsem,
            device_id={"section": section, "dp": dp}, device_id_type=MESH,
        )

    terms(1 - core, theirs)
    pl.semaphore_wait(barrier, n * groups - 1)
    swap = remote(theirs, arrived, pair_sem.at[0], pair_sem.at[1], partner, d)
    swap.start()
    terms(core, mine)
    swap.wait_recv()

    def across(c, i):
        bit = 1
        while bit < chips:
            if i & bit:
                c = c + bit * (1 - 2 * ((c // bit) % 2))
            bit *= 2
        return c

    k_chunk = k_half // chips
    sends = []
    for i in range(chips - 1, 0, -1):
        to = across(chip, i)
        ks = pl.ds(to * k_chunk, k_chunk)
        mine[ks] = mine[ks] + arrived[ks]
        copy = remote(mine.at[ks], pieces.at[i - 1], send_sem.at[i - 1], recv_sem.at[i - 1], 2 * to + core, d)
        copy.start()
        sends.append(copy)
    ks = pl.ds(chip * k_chunk, k_chunk)
    total = mine[ks] + arrived[ks]
    for i in range(1, chips):
        sends[chips - 1 - i].wait_recv()
        total = total + pieces[i - 1]

    own[...] = total

    per_group = n // groups
    q = core * chips + chip
    own_slot = q % per_group
    home = q // per_group
    at_home = home == d

    def col_copy(i):
        return remote(
            own, cols.at[own_slot, d], col_send.at[i], col_recv.at[own_slot, d], 2 * across(chip, i) + core, home
        )

    def pair_copy():
        return remote(own, cols.at[own_slot, d], col_send.at[0], col_recv.at[own_slot, d], partner, d)

    def row_copy(g):
        return remote(own, row.at[d], row_send.at[g], row_recv.at[d], q, g)

    for i in range(chips - 1, 0, -1):
        col_copy(i).start()

    @pl.when(at_home)
    def _():
        pair_copy().start()
        cols[own_slot, d] = own[...]

    @pl.when(jnp.logical_not(at_home))
    def _():
        col_copy(0).start()

    for g in range(groups):
        needed = home != g
        here = jnp.logical_and(q == s, d == g)

        @pl.when(jnp.logical_and(needed, jnp.logical_not(here)))
        def _():
            row_copy(g).start()

        @pl.when(jnp.logical_and(needed, here))
        def _():
            row[d] = own[...]

    def forward(j, g):
        return remote(cols.at[j, g], cols.at[j, g], fwd_send.at[j, g], col_recv.at[j, g], partner, d)

    for i in range(per_group):
        j = (chip + i) % per_group
        owner = d * per_group + j
        for g in range(groups):
            other = jnp.logical_or(owner != q, d != g)

            @pl.when(other)
            def _():
                forward(j, g).wait_recv()

            @pl.when(jnp.logical_and(other, owner // chips == core))
            def _():
                forward(j, g).start()

        for k in range(k_chunk):
            hi, lo = split(jnp.concatenate([cols[j, g, k] for g in range(groups)], axis=0))
            at = pl.multiple_of((j * k_chunk + k) * LANES, LANES)
            right[:, pl.ds(at, LANES)] = jnp.concatenate([hi, hi, lo], axis=0)

    for g in range(groups):

        @pl.when(jnp.logical_and(s // per_group != d, jnp.logical_or(q != s, d != g)))
        def _():
            remote(own, row.at[g], row_send.at[g], row_recv.at[g], q, d).wait_recv()

    @pl.when(s // per_group == d)
    def _():
        row[...] = cols[s % per_group]

    for k in range(k_chunk):
        hi, lo = split(jnp.concatenate([row[g, k] for g in range(groups)], axis=0) * scale)
        left[:, k * LANES:(k + 1) * LANES] = jnp.concatenate([hi, lo, hi], axis=0)

    hold.wait()
    swap.wait_send()
    for copy in sends:
        copy.wait_send()

    for i in range(1, chips):
        col_copy(i).wait_send()

    @pl.when(at_home)
    def _():
        pair_copy().wait_send()

    @pl.when(jnp.logical_not(at_home))
    def _():
        col_copy(0).wait_send()

    for g in range(groups):

        @pl.when(jnp.logical_and(home != g, jnp.logical_or(q != s, d != g)))
        def _():
            row_copy(g).wait_send()

    for j in range(per_group):
        owner = d * per_group + j
        for g in range(groups):

            @pl.when(jnp.logical_and(jnp.logical_or(owner != q, d != g), owner // chips == core))
            def _():
                forward(j, g).wait_send()


def gram_kernel(tiles, left, right, earlier, out, tile_v, sem):
    columns = right.shape[1] // tiles
    lhs = left[...].T
    copies = []
    for i in range(tiles):
        cs = slice(i * columns, (i + 1) * columns)
        tile_v[:, cs] = earlier[:, cs] + jnp.dot(lhs, right[:, cs], preferred_element_type=jnp.float32)
        copy = pltpu.make_async_copy(
            tile_v.at[:, pl.ds(i * columns, columns)], out.at[:, pl.ds(i * columns, columns)], sem.at[i]
        )
        copy.start()
        copies.append(copy)
    for copy in copies:
        copy.wait()


def per_device(activations, out_grads, proj_in, proj_out, earlier_gram):
    n = lax.axis_size("section")
    groups = lax.axis_size("dp")
    _, count, length, width = activations.shape
    _, draws, _, k_in = proj_in.shape
    k_out = proj_out.shape[2]
    tokens = count * length
    examples = count * groups
    scale = 1.0 / (length * n * draws) / examples
    row_width, col_width = earlier_gram.shape
    chips = n // 2
    k_half = k_out // 2
    k_chunk = k_half // chips
    per_group = n // groups
    any_spec = pl.BlockSpec(memory_space=pl.ANY)
    vmem_spec = pl.BlockSpec(memory_space=pltpu.VMEM)
    f32, bf16 = jnp.float32, jnp.bfloat16
    dma = pltpu.SemaphoreType.DMA

    left, right, held = pl.pallas_call(
        functools.partial(feature_kernel, n, groups, count, scale),
        out_shape=(
            pltpu.VMEM((3 * examples, row_width), bf16),
            pltpu.VMEM((3 * examples, col_width), bf16),
            pltpu.VMEM((row_width, col_width), f32),
        ),
        in_specs=[any_spec] * 5,
        out_specs=(vmem_spec, vmem_spec, vmem_spec),
        scratch_shapes=[
            pltpu.VMEM((tokens, width), bf16),
            pltpu.VMEM((tokens, width), bf16),
            pltpu.VMEM((draws, width, k_in), bf16),
            pltpu.VMEM((draws, k_out, width), bf16),
            pltpu.VMEM((tokens, draws * k_in), bf16),
            pltpu.VMEM((draws * k_out, tokens), bf16),
            pltpu.VMEM((k_half, count, k_in), f32),
            pltpu.VMEM((k_half, count, k_in), f32),
            pltpu.VMEM((k_half, count, k_in), f32),
            pltpu.VMEM((chips - 1, k_chunk, count, k_in), f32),
            pltpu.VMEM((k_chunk, count, k_in), f32),
            pltpu.VMEM((per_group, groups, k_chunk, count, k_in), f32),
            pltpu.VMEM((groups, k_chunk, count, k_in), f32),
            dma((2 * DEPTHS * (HALVES + 1),)),
            dma((2,)),
            dma((chips - 1,)),
            dma((chips - 1,)),
            dma((chips,)),
            dma((per_group, groups)),
            dma((per_group, groups)),
            dma((groups,)),
            dma((groups,)),
            dma,
        ],
        compiler_params=pltpu.CompilerParams(
            collective_id=0, has_side_effects=True, vmem_limit_bytes=52 << 20
        ),
        name="features",
    )(
        activations.reshape(tokens, width),
        out_grads.reshape(tokens, width),
        proj_in[0],
        proj_out[0],
        earlier_gram,
    )
    tiles = 8
    return pl.pallas_call(
        functools.partial(gram_kernel, tiles),
        out_shape=jax.ShapeDtypeStruct((row_width, col_width), f32),
        in_specs=[vmem_spec, vmem_spec, vmem_spec],
        out_specs=any_spec,
        scratch_shapes=[pltpu.VMEM((row_width, col_width), f32), dma((tiles,))],
        compiler_params=pltpu.CompilerParams(vmem_limit_bytes=28 << 20),
        name="gram",
    )(left, right, held)


def solution(mesh):
    return jax.shard_map(
        per_device,
        mesh=mesh,
        in_specs=(
            P("section", "dp", None, None),
            P("section", "dp", None, None),
            P("section", None, None, None),
            P("section", None, None, None),
            P("section", "dp"),
        ),
        out_specs=P("section", "dp"),
        check_vma=False,
    )
```

```python
import functools
import math

import jax
import jax.numpy as jnp
from jax import lax
from jax.experimental import pallas as pl
from jax.experimental.pallas import tpu as pltpu
from jax.sharding import PartitionSpec as P

MESH = pl.DeviceIdType.MESH
LANES = 128
HALVES = 2
DEPTHS = 1
WINDOW = 4


def split(x):
    hi = x.astype(jnp.bfloat16)
    lo = (x - hi.astype(jnp.float32)).astype(jnp.bfloat16)
    return hi, lo


def feature_kernel(
    n, groups, count, scale,
    act, grad, p_in, p_out, earlier,
    left, right, held,
    act_v, grad_v, in_v, out_v, low_in, low_out,
    mine, theirs, arrived, pieces, own, cols, row,
    load_sem, pair_sem, send_sem, recv_sem,
    col_send, col_recv, fwd_send, row_send, row_recv, held_sem,
):
    s = lax.axis_index("section")
    d = lax.axis_index("dp")
    chips = n // 2
    core = s % 2
    chip = s // 2
    partner = s + 1 - 2 * core

    draws, width, k_in = p_in.shape
    k_out = p_out.shape[1]
    tokens = act.shape[0]
    length = tokens // count
    rows = tokens // HALVES
    depth = width // DEPTHS

    loads = {}
    slot = 0
    for h in range(HALVES):
        for c in range(DEPTHS):
            cs = pl.ds(c * depth, depth)
            rs = pl.ds(h * rows, rows)
            wanted = []
            if h == 0:
                wanted.append(("p_in", p_in.at[:, cs], in_v.at[:, cs]))
            wanted.append(("act", act.at[rs, cs], act_v.at[rs, cs]))
            if h == 0:
                wanted.append(("p_out", p_out.at[:, :, cs], out_v.at[:, :, cs]))
            wanted.append(("grad", grad.at[rs, cs], grad_v.at[rs, cs]))
            for name, src, dst in wanted:
                copy = pltpu.make_async_copy(src, dst, load_sem.at[slot])
                loads[name, h, c] = copy
                slot += 1
    queue = list(loads.values())

    def take(copy):
        copy.wait()
        if queue:
            queue.pop(0).start()

    for _ in range(WINDOW):
        queue.pop(0).start()

    barrier = pltpu.get_barrier_semaphore()
    for g in range(groups):
        for i in range(n):
            if g or i:
                peer = {"section": (s + i) % n, "dp": (d + g) % groups}
                pl.semaphore_signal(barrier, inc=1, device_id=peer, device_id_type=MESH)

    for h in range(HALVES):
        rs = slice(h * rows, (h + 1) * rows)
        total_in = total_out = None
        for c in range(DEPTHS):
            cs = slice(c * depth, (c + 1) * depth)
            if h == 0:
                take(loads["p_in", h, c])
            take(loads["act", h, c])
            weights = jnp.concatenate([in_v[p, cs, :] for p in range(draws)], axis=1)
            term = jnp.dot(act_v[rs, cs], weights, preferred_element_type=jnp.float32)
            total_in = term if total_in is None else total_in + term
            if h == 0:
                take(loads["p_out", h, c])
            take(loads["grad", h, c])
            weights = out_v[:, :, cs].reshape(draws * k_out, depth)
            term = lax.dot_general(
                grad_v[rs, cs], weights, (((1,), (1,)), ((), ())), preferred_element_type=jnp.float32
            )
            total_out = term if total_out is None else total_out + term
        if h == HALVES - 1:
            hold = pltpu.make_async_copy(earlier, held, held_sem)
            hold.start()
        low_in[rs, :] = total_in.astype(jnp.bfloat16)
        low_out[:, rs] = total_out.T.astype(jnp.bfloat16)

    k_half = k_out // 2

    def terms(which, into):
        for e in range(count):
            ts = slice(e * length, (e + 1) * length)
            value = None
            for p in range(draws):
                start = pl.multiple_of(p * k_out + which * k_half, k_half)
                term = jnp.dot(
                    low_out[pl.ds(start, k_half), ts],
                    low_in[ts, p * k_in:(p + 1) * k_in],
                    preferred_element_type=jnp.float32,
                )
                value = term if value is None else value + term
            into[:, e, :] = value

    def remote(src, dst, ssem, rsem, section, dp):
        return pltpu.make_async_remote_copy(
            src_ref=src, dst_ref=dst, send_sem=ssem, recv_sem=rsem,
            device_id={"section": section, "dp": dp}, device_id_type=MESH,
        )

    terms(1 - core, theirs)
    pl.semaphore_wait(barrier, n * groups - 1)
    swap = remote(theirs, arrived, pair_sem.at[0], pair_sem.at[1], partner, d)
    swap.start()
    terms(core, mine)
    swap.wait_recv()

    def across(c, i):
        bit = 1
        while bit < chips:
            if i & bit:
                c = c + bit * (1 - 2 * ((c // bit) % 2))
            bit *= 2
        return c

    k_chunk = k_half // chips
    sends = []
    for i in range(chips - 1, 0, -1):
        to = across(chip, i)
        ks = pl.ds(to * k_chunk, k_chunk)
        mine[ks] = mine[ks] + arrived[ks]
        copy = remote(mine.at[ks], pieces.at[i - 1], send_sem.at[i - 1], recv_sem.at[i - 1], 2 * to + core, d)
        copy.start()
        sends.append(copy)
    ks = pl.ds(chip * k_chunk, k_chunk)
    total = mine[ks] + arrived[ks]
    for i in range(1, chips):
        sends[chips - 1 - i].wait_recv()
        total = total + pieces[i - 1]

    own[...] = total

    per_group = n // groups
    q = core * chips + chip
    own_slot = q % per_group
    home = q // per_group
    at_home = home == d

    def col_copy(i):
        return remote(
            own, cols.at[own_slot, d], col_send.at[i], col_recv.at[own_slot, d], 2 * across(chip, i) + core, home
        )

    def pair_copy():
        return remote(own, cols.at[own_slot, d], col_send.at[0], col_recv.at[own_slot, d], partner, d)

    def row_copy(g):
        return remote(own, row.at[d], row_send.at[g], row_recv.at[d], q, g)

    for i in range(chips - 1, 0, -1):
        col_copy(i).start()

    @pl.when(at_home)
    def _():
        pair_copy().start()
        cols[own_slot, d] = own[...]

    @pl.when(jnp.logical_not(at_home))
    def _():
        col_copy(0).start()

    for g in range(groups):
        needed = home != g
        here = jnp.logical_and(q == s, d == g)

        @pl.when(jnp.logical_and(needed, jnp.logical_not(here)))
        def _():
            row_copy(g).start()

        @pl.when(jnp.logical_and(needed, here))
        def _():
            row[d] = own[...]

    def forward(j, g):
        return remote(cols.at[j, g], cols.at[j, g], fwd_send.at[j, g], col_recv.at[j, g], partner, d)

    for i in range(per_group):
        j = across(chip, i) % per_group
        owner = d * per_group + j
        for g in range(groups):
            other = jnp.logical_or(owner != q, d != g)

            @pl.when(other)
            def _():
                forward(j, g).wait_recv()

            @pl.when(jnp.logical_and(other, owner // chips == core))
            def _():
                forward(j, g).start()

        for k in range(k_chunk):
            hi, lo = split(jnp.concatenate([cols[j, g, k] for g in range(groups)], axis=0))
            at = pl.multiple_of((j * k_chunk + k) * LANES, LANES)
            right[:, pl.ds(at, LANES)] = jnp.concatenate([hi, hi, lo], axis=0)

    for g in range(groups):

        @pl.when(jnp.logical_and(s // per_group != d, jnp.logical_or(q != s, d != g)))
        def _():
            remote(own, row.at[g], row_send.at[g], row_recv.at[g], q, d).wait_recv()

    @pl.when(s // per_group == d)
    def _():
        row[...] = cols[s % per_group]

    for k in range(k_chunk):
        hi, lo = split(jnp.concatenate([row[g, k] for g in range(groups)], axis=0) * scale)
        left[:, k * LANES:(k + 1) * LANES] = jnp.concatenate([hi, lo, hi], axis=0)

    hold.wait()
    swap.wait_send()
    for copy in sends:
        copy.wait_send()

    for i in range(1, chips):
        col_copy(i).wait_send()

    @pl.when(at_home)
    def _():
        pair_copy().wait_send()

    @pl.when(jnp.logical_not(at_home))
    def _():
        col_copy(0).wait_send()

    for g in range(groups):

        @pl.when(jnp.logical_and(home != g, jnp.logical_or(q != s, d != g)))
        def _():
            row_copy(g).wait_send()

    for j in range(per_group):
        owner = d * per_group + j
        for g in range(groups):

            @pl.when(jnp.logical_and(jnp.logical_or(owner != q, d != g), owner // chips == core))
            def _():
                forward(j, g).wait_send()


def gram_kernel(tiles, left, right, earlier, out, tile_v, sem):
    columns = right.shape[1] // tiles
    lhs = left[...].T
    copies = []
    for i in range(tiles):
        cs = slice(i * columns, (i + 1) * columns)
        tile_v[:, cs] = earlier[:, cs] + jnp.dot(lhs, right[:, cs], preferred_element_type=jnp.float32)
        copy = pltpu.make_async_copy(
            tile_v.at[:, pl.ds(i * columns, columns)], out.at[:, pl.ds(i * columns, columns)], sem.at[i]
        )
        copy.start()
        copies.append(copy)
    for copy in copies:
        copy.wait()


def per_device(activations, out_grads, proj_in, proj_out, earlier_gram):
    n = lax.axis_size("section")
    groups = lax.axis_size("dp")
    _, count, length, width = activations.shape
    _, draws, _, k_in = proj_in.shape
    k_out = proj_out.shape[2]
    tokens = count * length
    examples = count * groups
    scale = 1.0 / (length * n * draws) / examples
    row_width, col_width = earlier_gram.shape
    chips = n // 2
    k_half = k_out // 2
    k_chunk = k_half // chips
    per_group = n // groups
    any_spec = pl.BlockSpec(memory_space=pl.ANY)
    vmem_spec = pl.BlockSpec(memory_space=pltpu.VMEM)
    f32, bf16 = jnp.float32, jnp.bfloat16
    dma = pltpu.SemaphoreType.DMA

    left, right, held = pl.pallas_call(
        functools.partial(feature_kernel, n, groups, count, scale),
        out_shape=(
            pltpu.VMEM((3 * examples, row_width), bf16),
            pltpu.VMEM((3 * examples, col_width), bf16),
            pltpu.VMEM((row_width, col_width), f32),
        ),
        in_specs=[any_spec] * 5,
        out_specs=(vmem_spec, vmem_spec, vmem_spec),
        scratch_shapes=[
            pltpu.VMEM((tokens, width), bf16),
            pltpu.VMEM((tokens, width), bf16),
            pltpu.VMEM((draws, width, k_in), bf16),
            pltpu.VMEM((draws, k_out, width), bf16),
            pltpu.VMEM((tokens, draws * k_in), bf16),
            pltpu.VMEM((draws * k_out, tokens), bf16),
            pltpu.VMEM((k_half, count, k_in), f32),
            pltpu.VMEM((k_half, count, k_in), f32),
            pltpu.VMEM((k_half, count, k_in), f32),
            pltpu.VMEM((chips - 1, k_chunk, count, k_in), f32),
            pltpu.VMEM((k_chunk, count, k_in), f32),
            pltpu.VMEM((per_group, groups, k_chunk, count, k_in), f32),
            pltpu.VMEM((groups, k_chunk, count, k_in), f32),
            dma((2 * DEPTHS * (HALVES + 1),)),
            dma((2,)),
            dma((chips - 1,)),
            dma((chips - 1,)),
            dma((chips,)),
            dma((per_group, groups)),
            dma((per_group, groups)),
            dma((groups,)),
            dma((groups,)),
            dma,
        ],
        compiler_params=pltpu.CompilerParams(
            collective_id=0, has_side_effects=True, vmem_limit_bytes=52 << 20
        ),
        name="features",
    )(
        activations.reshape(tokens, width),
        out_grads.reshape(tokens, width),
        proj_in[0],
        proj_out[0],
        earlier_gram,
    )
    tiles = 8
    return pl.pallas_call(
        functools.partial(gram_kernel, tiles),
        out_shape=jax.ShapeDtypeStruct((row_width, col_width), f32),
        in_specs=[vmem_spec, vmem_spec, vmem_spec],
        out_specs=any_spec,
        scratch_shapes=[pltpu.VMEM((row_width, col_width), f32), dma((tiles,))],
        compiler_params=pltpu.CompilerParams(vmem_limit_bytes=28 << 20),
        name="gram",
    )(left, right, held)


def solution(mesh):
    return jax.shard_map(
        per_device,
        mesh=mesh,
        in_specs=(
            P("section", "dp", None, None),
            P("section", "dp", None, None),
            P("section", None, None, None),
            P("section", None, None, None),
            P("section", "dp"),
        ),
        out_specs=P("section", "dp"),
        check_vma=False,
    )
```
